32 devices in a mesh: wide: 8 (over y, x, core), narrow: 4 (over z).
Axes of the slice: x: 2, y: 2, z: 4, core: 2. Of those that a mesh axis runs over, the one named last changes fastest.
Arguments:
- events: bfloat16 [8192, 1024], P('wide'), may hold values from -36 to 36
- lengths: int32 [24], replicated, may hold values from 1 to 2048, 8192 in all
- in_gain: float32 [1024], replicated, may hold values from 0.1 to 1.9
- w_uvqk: bfloat16 [1024, 8, 512], P(None, 'narrow'), may hold values from -2 to 2, as said below
- out_gain: float32 [8, 128], P('narrow'), may hold values from 0.1 to 1.9
- w_out: bfloat16 [8, 128, 1024], P('narrow'), may hold values from -0.25 to 0.25
Outputs:
- layer_out: bfloat16 [8192, 1024], P('wide', 'narrow')
The draws below stay inside these ranges and needn't reach their ends.
Inputs may be any that keep to these rules, and one draw needn't show every extreme that they name: `w_uvqk`: projection weights.
All inputs are finite; a program needn't handle non-finite values.
Results may differ from the reference program's by a relative error of at most 0.0036.
Values may be sent and summed in bfloat16 or wider, within the bound.
A program may use at most 64 MiB of HBM per device.

```python
import math
import jax
import jax.numpy as jnp
import numpy as np
from jax import lax

D = 1024
H = 8
DH = 128
USERS = 24
ROWS_W = 1024
TOTAL = 8192
MOST = 2048


def draw_events(key, part):
    key_rows, key_cols, key_dirs, key_offsets, key_spread, key_noise = jax.random.split(jax.random.fold_in(key, 7), 6)
    row_scale = jnp.exp(jax.random.uniform(key_rows, (TOTAL, 1), jnp.float32, jnp.log(0.3), jnp.log(3.0)))
    col_scale = jnp.exp(jax.random.uniform(key_cols, (1, D), jnp.float32, jnp.log(0.3), jnp.log(3.0)))
    segment_len = max(ROWS_W * 3 // 8, 1)
    segment_count = TOTAL // segment_len + 1
    segment_of = (jnp.arange(TOTAL, dtype=jnp.int32) // segment_len).astype(jnp.int32)
    directions = jnp.clip(jax.random.normal(key_dirs, (3, D), jnp.float32), -3.0, 3.0)
    offsets = 0.6 * jnp.clip(jax.random.normal(key_offsets, (segment_count, 3), jnp.float32), -3.0, 3.0)
    spread = 0.45 * jnp.clip(jax.random.normal(key_spread, (TOTAL, 3), jnp.float32), -3.0, 3.0)
    noise = 0.6 * jnp.clip(jax.random.normal(key_noise, (TOTAL, D), jnp.float32), -4.0, 4.0)
    coefficients = jnp.take(offsets, segment_of, axis=0) + spread
    inner = coefficients[:, 0:1] * directions[0:1] + coefficients[:, 1:2] * directions[1:2]
    inner = inner + coefficients[:, 2:3] * directions[2:3] + noise
    inner = jnp.clip(inner, -4.0, 4.0)
    return (inner * row_scale * col_scale).astype(jnp.bfloat16)


def draw_w_uvqk(key, part):
    key_base, key_own = jax.random.split(jax.random.fold_in(key, 11), 2)
    base = jnp.clip(jax.random.normal(key_base, (D, H, 4 * DH), jnp.float32), -5.0, 5.0)
    own = jnp.clip(jax.random.normal(key_own, (D, H, DH), jnp.float32), -5.0, 5.0)
    narrow_scale = D ** (-0.5)
    broad_scale = (3.0 / D) ** 0.5
    gate_value = base[:, :, :2 * DH] * narrow_scale
    query_part = base[:, :, 2 * DH:3 * DH]
    key_part = 0.9 * query_part + 0.44 * own
    whole = jnp.concatenate([gate_value, query_part * broad_scale, key_part * broad_scale], axis=2)
    return whole.astype(jnp.bfloat16)


def with_spikes(array, rng, source, target, blocks, factor):
    owner, partner = [(jnp.arange(array.shape[position]) // (array.shape[position] // blocks)).reshape([-1 if axis == position else 1 for axis in range(array.ndim)]) for position in (source, target)]
    chosen = jax.random.permutation(rng, blocks)[partner]
    strong = (owner == chosen) | (owner == (partner + blocks // 2) % blocks)
    return jnp.where(strong, factor * array, array)


def shard_levels(stream_key, extent, cuts, low, top_value):
    factor_of = 1.0
    for axis_at, shards_of in cuts:
        steps = jax.random.uniform(jax.random.fold_in(jax.random.fold_in(stream_key, 6), axis_at), (shards_of,), jnp.float32, low / len(cuts), top_value / len(cuts))
        factor_of = factor_of * jnp.repeat(jnp.exp(steps), extent[axis_at] // shards_of).reshape((-1,) + (1,) * (len(extent) - 1 - axis_at))
    return factor_of


def profile(count, total, bound, lean):
    loads = [(1 << 20) // math.isqrt(grade ** lean) + 1 for grade in range(2, count + 1)]
    spare, given = total - bound - (count - 1), [1] * (count - 1)
    while spare > 0:
        movable = [i for i in range(count - 1) if given[i] < bound]
        mass, budget = sum([loads[i] for i in movable]), spare
        for i in movable:
            more = min(bound - given[i], max(1, budget * loads[i] // mass), spare)
            given[i] = given[i] + more
            spare = spare - more
    return np.array([bound] + given)


def ragged_sizes(key, amount, total, limit, skew):
    if amount == 2:
        one = jax.random.randint(key, (), max(1, total - limit), min(limit, total - 1) + 1)
        return jnp.stack([one, total - one])
    tallies = jnp.asarray(profile(amount, total, limit, skew), jnp.int32)
    couples = (amount - 1) // 2
    donor, receiver = tallies[1:1 + 2 * couples:2], tallies[2:2 + 2 * couples:2]
    slack = jnp.minimum(donor - 1, limit - receiver)
    passed = jax.random.randint(jax.random.fold_in(key, 1), (couples,), 0, 1 << 20) % (slack + 1)
    tallies = tallies.at[1:1 + 2 * couples:2].set(donor - passed).at[2:2 + 2 * couples:2].set(receiver + passed)
    return tallies[jax.random.permutation(jax.random.fold_in(key, 2), amount)]


def noise_with(stream_key, extent, scale, limit, cuts, heavy, kind=jnp.bfloat16):
    values = scale * jax.random.normal(stream_key, extent, jnp.float32)
    if cuts:
        values = values * shard_levels(stream_key, extent, cuts, -0.22, 0.18)
    return jnp.clip(with_spikes(values, jax.random.fold_in(stream_key, 3), *heavy), -limit, limit).astype(kind)


def setup_inputs(seed: int = 0) -> dict:
    streams_of = jax.random.split(jax.random.key(seed), 7)
    return {
        "events": draw_events(jax.random.fold_in(streams_of[6], 71), 0),
        "lengths": ragged_sizes(streams_of[1], USERS, TOTAL, MOST, 2).astype(jnp.int32),
        "in_gain": jnp.clip(1.0 + 0.18 * jax.random.normal(streams_of[2], (D,), jnp.float32), 0.1, 1.9),
        "w_uvqk": draw_w_uvqk(jax.random.fold_in(streams_of[6], 71), 0),
        "out_gain": jnp.clip(1.0 + 0.18 * jax.random.normal(streams_of[4], (H, DH), jnp.float32), 0.1, 1.9),
        "w_out": noise_with(streams_of[5], (H, DH, D), (H * DH) ** -0.5, 0.25, ((0, 4),), (0, 2, 4, 2.0)),
    }


def reference(events, lengths, in_gain, w_uvqk, out_gain, w_out):
    events_f = events.astype(jnp.float32)
    average = lax.optimization_barrier(jnp.mean(events_f, axis=-1, keepdims=True))
    variance = lax.optimization_barrier(jnp.mean((events_f - average) ** 2, axis=-1, keepdims=True))
    normed = ((events_f - average) * lax.rsqrt(variance + 1e-05) * in_gain).astype(jnp.bfloat16)
    projected = jnp.dot(normed, w_uvqk.reshape(D, H * 4 * DH), preferred_element_type=jnp.float32)
    projected = jax.nn.silu(projected).reshape(TOTAL, H, 4 * DH).astype(jnp.bfloat16)
    update_gate = projected[:, :, :DH]
    values_all = projected[:, :, DH:2 * DH]
    queries = projected[:, :, 2 * DH:3 * DH]
    keys_all = projected[:, :, 3 * DH:]
    user_ends = jnp.cumsum(lengths).astype(jnp.int32)
    positions = jnp.arange(TOTAL, dtype=jnp.int32)
    owners = lax.optimization_barrier(jnp.sum((user_ends[None, :] <= positions[:, None]).astype(jnp.int32), axis=1))
    query_rows = min(512, TOTAL)
    window = min(TOTAL, MOST + query_rows)
    scaling = DH ** (-0.5)

    def query_block(block_index):
        query_start = block_index * query_rows
        key_start = jnp.clip(query_start + query_rows - window, 0, TOTAL - window).astype(jnp.int32)
        query_part = lax.dynamic_slice_in_dim(queries, query_start, query_rows, 0).astype(jnp.float32)
        query_pos = lax.dynamic_slice_in_dim(positions, query_start, query_rows, 0)
        query_user = lax.dynamic_slice_in_dim(owners, query_start, query_rows, 0)
        key_part = lax.dynamic_slice_in_dim(keys_all, key_start, window, 0).astype(jnp.float32)
        value_part = lax.dynamic_slice_in_dim(values_all, key_start, window, 0).astype(jnp.float32)
        key_pos = lax.dynamic_slice_in_dim(positions, key_start, window, 0)
        key_user = lax.dynamic_slice_in_dim(owners, key_start, window, 0)
        scores = jnp.einsum('rhc,khc->hrk', query_part, key_part) * scaling
        allowed = (key_user[None, :] == query_user[:, None]) & (key_pos[None, :] <= query_pos[:, None])
        weights = jnp.where(allowed[None], jax.nn.silu(scores), 0.0).astype(jnp.bfloat16)
        return jnp.einsum('hrk,khc->rhc', weights.astype(jnp.float32), value_part)
    attended = lax.map(query_block, jnp.arange(TOTAL // query_rows, dtype=jnp.int32))
    attended = attended.reshape(TOTAL, H, DH)
    centre = lax.optimization_barrier(jnp.mean(attended, axis=-1, keepdims=True))
    deviation = lax.optimization_barrier(jnp.mean((attended - centre) ** 2, axis=-1, keepdims=True))
    gated = (attended - centre) * lax.rsqrt(deviation + 1e-05) * out_gain[None] * update_gate.astype(jnp.float32)
    gated = gated.astype(jnp.bfloat16)
    branch = jnp.dot(gated.reshape(TOTAL, H * DH), w_out.reshape(H * DH, D), preferred_element_type=jnp.float32)
    return (events_f + branch).astype(jnp.bfloat16)
```

```python
import functools

import jax
import jax.numpy as jnp
from jax import lax
from jax.experimental import pallas as pl
from jax.experimental.pallas import tpu as pltpu
from jax.sharding import PartitionSpec as P

MESH = pl.DeviceIdType.MESH
F32 = jnp.float32
BF16 = jnp.bfloat16


def half_silu(half):
    return half + half * jnp.tanh(half)


def kernel(
    wide, narrow, reach, parts,
    len_ref, ev_ref, gain_ref, w_ref, og_ref, wo_ref, out_ref,
    normed, ubuf, qbuf, kvbuf, acc, start_ref, gown, gbuf, wcols, oacc,
    kv_send, kv_recv, g_send, g_recv, w_send, w_recv,
):
    me_w = lax.axis_index("wide")
    me_z = lax.axis_index("narrow")
    rows, width = ev_ref.shape
    heads, size = og_ref.shape
    share = out_ref.shape[1]
    users = len_ref.shape[0]
    tile = min(256, rows)
    tiles = rows // tile
    part = rows // parts

    barrier = pltpu.get_barrier_semaphore()

    @pl.when(me_w > 0)
    def _():
        pl.semaphore_signal(barrier, inc=1, device_id=(me_w - 1, me_z), device_id_type=MESH)

    @pl.when(me_w < wide - 1)
    def _():
        pl.semaphore_signal(barrier, inc=1, device_id=(me_w + 1, me_z), device_id_type=MESH)

    for d in range(1, narrow):
        @pl.when(me_z + d < narrow)
        def _():
            pl.semaphore_signal(barrier, inc=1, device_id=(me_w, me_z + d), device_id_type=MESH)

        @pl.when(me_z - d >= 0)
        def _():
            pl.semaphore_signal(barrier, inc=1, device_id=(me_w, me_z - d), device_id_type=MESH)

    def w_copy(direction, d):
        peer = me_z + d if direction == 0 else me_z - d
        return pltpu.make_async_remote_copy(
            src_ref=wo_ref.at[:, pl.ds(pl.multiple_of(peer * share, share), share)],
            dst_ref=wcols.at[direction, d - 1],
            send_sem=w_send.at[direction, d - 1],
            recv_sem=w_recv.at[direction, d - 1],
            device_id=(me_w, peer),
            device_id_type=MESH,
        )

    def w_landed(direction, d):
        return pltpu.make_async_remote_copy(
            src_ref=wcols.at[direction, d - 1],
            dst_ref=wcols.at[direction, d - 1],
            send_sem=w_send.at[direction, d - 1],
            recv_sem=w_recv.at[direction, d - 1],
            device_id=(me_w, me_z),
            device_id_type=MESH,
        )

    def kv_copy(step, h):
        return pltpu.make_async_remote_copy(
            src_ref=kvbuf.at[step - 1, h],
            dst_ref=kvbuf.at[step, h],
            send_sem=kv_send.at[step - 1, h],
            recv_sem=kv_recv.at[step - 1, h],
            device_id=(me_w + 1, me_z),
            device_id_type=MESH,
        )

    def kv_goes(step):
        return (me_w >= step - 1) & (me_w < wide - 1)

    def kv_start(step, h):
        @pl.when(kv_goes(step))
        def _():
            kv_copy(step, h).start()

    def g_copy(direction, d, c):
        h, r = c // parts, c % parts
        rs = pl.ds(r * part, part)
        src = gown.at[h, rs] if d == 1 else gbuf.at[direction, d - 2, h, rs]
        peer = me_z + 1 if direction == 0 else me_z - 1
        return pltpu.make_async_remote_copy(
            src_ref=src,
            dst_ref=gbuf.at[direction, d - 1, h, rs],
            send_sem=g_send.at[direction, d - 1, c],
            recv_sem=g_recv.at[direction, d - 1, c],
            device_id=(me_w, peer),
            device_id_type=MESH,
        )

    def g_goes(direction, d):
        if direction == 0:
            return (me_z >= d - 1) & (me_z < narrow - 1)
        return (me_z + d - 1 < narrow) & (me_z > 0)

    def g_start(direction, d, c):
        @pl.when(g_goes(direction, d))
        def _():
            g_copy(direction, d, c).start()

    def has(direction, d):
        return me_z >= d if direction == 0 else me_z + d < narrow

    ln_tile = min(128, rows)

    def ln(t, _):
        rs = pl.ds(pl.multiple_of(t * ln_tile, ln_tile), ln_tile)
        x = ev_ref[rs, :].astype(F32)
        x = x - jnp.mean(x, axis=1, keepdims=True)
        var = jnp.mean(x * x, axis=1, keepdims=True)
        normed[rs, :] = (x * lax.rsqrt(var + 1e-5) * gain_ref[...]).astype(BF16)
        return 0

    lax.fori_loop(0, rows // ln_tile, ln, 0)

    def project(h):
        def body(t, _):
            rs = pl.ds(pl.multiple_of(t * tile, tile), tile)
            p = jnp.dot(
                normed[rs, :], w_ref[:, h * 4 * size:(h + 1) * 4 * size],
                preferred_element_type=F32,
            )
            p = half_silu(p * 0.5).astype(BF16)
            ubuf[h, rs, :] = p[:, :size]
            kvbuf[0, h, 1, rs, :] = p[:, size:2 * size]
            qbuf[h, rs, :] = p[:, 2 * size:3 * size]
            kvbuf[0, h, 0, rs, :] = p[:, 3 * size:]
            return 0

        lax.fori_loop(0, tiles, body, 0)

    project(0)

    greeted = (
        jnp.where(me_w > 0, 1, 0) + jnp.where(me_w < wide - 1, 1, 0) + (narrow - 1)
    )
    pl.semaphore_wait(barrier, greeted)
    kv_start(1, 0)
    for d in range(1, narrow):
        @pl.when(me_z + d < narrow)
        def _():
            w_copy(0, d).start()

        @pl.when(me_z - d >= 0)
        def _():
            w_copy(1, d).start()

    for h in range(1, heads):
        project(h)

    lane = lax.broadcasted_iota(jnp.int32, (8, 128), 1)
    ends = jnp.zeros((8, 128), jnp.int32)
    for u in range(users):
        ends = ends + jnp.where(lane >= u, len_ref[u], 0)
    ends = jnp.where(lane < users, ends, jnp.int32(2 ** 30))[:1]
    first = me_w * rows

    def starts(t, _):
        rs = pl.ds(pl.multiple_of(t * tile, tile), tile)
        at = first + t * tile + lax.broadcasted_iota(jnp.int32, (tile, 128), 0)
        begun = jnp.max(jnp.where(ends <= at, ends, 0), axis=1, keepdims=True)
        start_ref[rs, :] = jnp.broadcast_to(begun - first, (tile, 128))
        return 0

    lax.fori_loop(0, tiles, starts, 0)
    scale = 0.5 * size ** (-0.5)

    def attend(step, h, lo=0, hi=None):
        def body(t, _):
            rs = pl.ds(pl.multiple_of(t * tile, tile), tile)
            s = lax.dot_general(
                qbuf[h, rs, :], kvbuf[step, h, 0],
                (((1,), (1,)), ((), ())), preferred_element_type=F32,
            )
            weights = half_silu(s * scale)
            key = lax.broadcasted_iota(jnp.int32, (1, rows), 1) - step * rows
            begun = start_ref[rs, :][:, :1]
            allowed = key >= begun
            if step == 0:
                query = t * tile + lax.broadcasted_iota(jnp.int32, (tile, 1), 0)
                allowed = allowed & (key <= query)
            weights = jnp.where(allowed, weights, 0.0).astype(BF16)
            out = jnp.dot(weights, kvbuf[step, h, 1], preferred_element_type=F32)
            if step == 0:
                acc[h, rs, :] = out
            else:
                acc[h, rs, :] += out
            return 0

        lax.fori_loop(lo, tiles if hi is None else hi, body, 0)

    def attend_far(step, h, lo=0, hi=None):
        @pl.when(me_w >= step)
        def _():
            attend(step, h, lo, hi)

    def kv_wait(step, h):
        @pl.when(me_w >= step)
        def _():
            kv_copy(step, h).wait_recv()

    def gate(h, lo, hi):
        def body(t, _):
            rs = pl.ds(pl.multiple_of(t * tile, tile), tile)
            a = acc[h, rs, :]
            a = a - jnp.mean(a, axis=1, keepdims=True)
            var = jnp.mean(a * a, axis=1, keepdims=True)
            g = a * lax.rsqrt(var + 1e-5) * og_ref[h:h + 1, :]
            gown[h, rs, :] = (g * ubuf[h, rs, :].astype(F32)).astype(BF16)
            return 0

        lax.fori_loop(lo, hi, body, 0)

    def finish(h):
        per = tiles // parts
        for r in range(parts):
            attend_far(reach, h, r * per, (r + 1) * per)
            gate(h, r * per, (r + 1) * per)
            for direction in range(2):
                g_start(direction, 1, h * parts + r)

    def own_cols(t):
        rs = pl.ds(pl.multiple_of(t * tile, tile), tile)
        cols = pl.ds(pl.multiple_of(me_z * share, share), share)
        return rs, cols

    kv_wait(1, 0)
    for step in range(2, min(reach, 2) + 1):
        kv_start(step, 0)
    for h in range(1, heads):
        kv_start(1, h)
    for h in range(heads):
        attend(0, h)
    attend_far(1, 0)
    for step in range(2, reach + 1):
        kv_wait(step, 0)
        if step < reach:
            kv_start(step + 1, 0)
        if step == 2:
            for h in range(1, heads):
                kv_wait(1, h)
                kv_start(2, h)
        if step < reach:
            attend_far(step, 0)

    def residual(t, _):
        rs, cols = own_cols(t)
        oacc[rs, :] = ev_ref[rs, cols].astype(F32)
        return 0

    finish(0)
    lax.fori_loop(0, tiles, residual, 0)
    for d in range(1, narrow):
        for direction in range(2):
            @pl.when(has(direction, d))
            def _():
                w_landed(direction, d).wait_recv()

    def relay(d, c):
        for direction in range(2):
            @pl.when(has(direction, d))
            def _():
                g_copy(direction, d, c).wait_recv()
            if d < narrow - 1:
                g_start(direction, d + 1, c)

    def gather_mul(d, c):
        h, r = c // parts, c % parts
        for direction in range(2):
            @pl.when(has(direction, d))
            def _():
                rs = pl.ds(r * part, part)
                oacc[rs, :] += jnp.dot(
                    gbuf[direction, d - 1, h, rs, :],
                    wcols[direction, d - 1, h * size:(h + 1) * size, :],
                    preferred_element_type=F32,
                )

    def own_mul(h):
        def body(t, _):
            rs, cols = own_cols(t)
            oacc[rs, :] += jnp.dot(
                gown[h, rs, :], wo_ref[h * size:(h + 1) * size, cols],
                preferred_element_type=F32,
            )
            return 0

        lax.fori_loop(0, tiles, body, 0)

    own_mul(0)
    done = set()
    for h in range(1, heads):
        attend_far(1, h)
        for c in range((h - 1) * parts, h * parts):
            relay(1, c)
            gather_mul(1, c)
            done.add((1, c))
        for step in range(2, reach + 1):
            kv_wait(step, h)
            if step < reach:
                kv_start(step + 1, h)
                attend_far(step, h)
        finish(h)
        own_mul(h)
    left = [
        (d * parts + c, d, c)
        for d in range(1, narrow) for c in range(heads * parts) if (d, c) not in done
    ]
    for _, d, c in sorted(left):
        relay(d, c)
        gather_mul(d, c)

    def store(t, _):
        rs = pl.ds(pl.multiple_of(t * tile, tile), tile)
        out_ref[rs, :] = oacc[rs, :].astype(out_ref.dtype)
        return 0

    lax.fori_loop(0, tiles, store, 0)

    for step in range(1, reach + 1):
        @pl.when(kv_goes(step))
        def _():
            for h in range(heads):
                kv_copy(step, h).wait_send()
    for d in range(1, narrow):
        @pl.when(me_z + d < narrow)
        def _():
            w_copy(0, d).wait_send()

        @pl.when(me_z - d >= 0)
        def _():
            w_copy(1, d).wait_send()

        for direction in range(2):
            @pl.when(g_goes(direction, d))
            def _():
                for c in range(heads * parts):
                    g_copy(direction, d, c).wait_send()


def solution(mesh):
    wide, narrow = mesh.shape["wide"], mesh.shape["narrow"]
    reach = wide // 4
    parts = 2

    def on_device(events, lengths, in_gain, w_uvqk, out_gain, w_out):
        rows, width = events.shape
        heads, size = out_gain.shape
        share = w_out.shape[2] // narrow
        chunks = heads * parts
        vmem = pl.BlockSpec(memory_space=pltpu.VMEM)
        return pl.pallas_call(
            functools.partial(kernel, wide, narrow, reach, parts),
            out_shape=jax.ShapeDtypeStruct((rows, share), BF16),
            in_specs=[pl.BlockSpec(memory_space=pltpu.SMEM)] + [vmem] * 5,
            out_specs=vmem,
            scratch_shapes=[
                pltpu.VMEM((rows, width), BF16),
                pltpu.VMEM((heads, rows, size), BF16),
                pltpu.VMEM((heads, rows, size), BF16),
                pltpu.VMEM((reach + 1, heads, 2, rows, size), BF16),
                pltpu.VMEM((heads, rows, size), F32),
                pltpu.VMEM((rows, 128), jnp.int32),
                pltpu.VMEM((heads, rows, size), BF16),
                pltpu.VMEM((2, narrow - 1, heads, rows, size), BF16),
                pltpu.VMEM((2, narrow - 1, heads * size, share), BF16),
                pltpu.VMEM((rows, share), F32),
                pltpu.SemaphoreType.DMA((reach, heads)),
                pltpu.SemaphoreType.DMA((reach, heads)),
                pltpu.SemaphoreType.DMA((2, narrow - 1, chunks)),
                pltpu.SemaphoreType.DMA((2, narrow - 1, chunks)),
                pltpu.SemaphoreType.DMA((2, narrow - 1)),
                pltpu.SemaphoreType.DMA((2, narrow - 1)),
            ],
            compiler_params=pltpu.CompilerParams(
                collective_id=0, has_side_effects=True,
                vmem_limit_bytes=60 * 1024 * 1024,
            ),
        )(
            lengths, events, in_gain.reshape(1, width),
            w_uvqk.reshape(width, heads * 4 * size), out_gain,
            w_out.reshape(heads * size, w_out.shape[2]),
        )

    in_specs = (
        P("wide", None),
        P(),
        P(),
        P(None, "narrow", None),
        P("narrow", None),
        P("narrow", None, None),
    )
    return jax.shard_map(
        on_device, mesh=mesh, in_specs=in_specs, out_specs=P("wide", "narrow"), check_vma=False
    )
```
